32 devices in a mesh: lat: 4 (over y, x), lon: 8 (over z, core).
Axes of the slice: x: 2, y: 2, z: 4, core: 2. Of those that a mesh axis runs over, the one named last changes fastest.
Arguments:
- queries: bfloat16 [64, 64, 768], P('lat', 'lon'), may hold values from -8 to 8
- key_vectors: bfloat16 [64, 64, 768], P('lat', 'lon'), may hold values from -8 to 8
- value_vectors: bfloat16 [64, 64, 768], P('lat', 'lon'), may hold values from -12 to 12
- upstream: bfloat16 [64, 64, 768], P('lat', 'lon'), may hold values from -6 to 6
- w_out: bfloat16 [768, 768], replicated, may hold values from -0.21875 to 0.21875
- neighbours: int32 [8, 8, 4], replicated, may hold values from 0 to 63, as said below
- counts: int32 [8, 8], replicated, may hold values from 2 to 4, as said below
Outputs:
- mixed_out: bfloat16 [64, 64, 768], P('lat', 'lon')
- q_grad: bfloat16 [64, 64, 768], P('lat', 'lon')
- k_grad: bfloat16 [64, 64, 768], P('lat', 'lon')
- v_grad: bfloat16 [64, 64, 768], P('lat', 'lon')
- w_grad: float32 [768, 768], replicated
The draws below stay inside these ranges and needn't reach their ends.
Inputs may be any that keep to these rules, and one draw needn't show every extreme that they name: `neighbours`: entry s of block (i, j) names a block i2 * 8 + j2 with i2 within one of i and j2 within one of j around the longitude circle; slot 0 names the block itself, the entries of slots below counts[i, j] are distinct, and the slots at or beyond counts[i, j] name the block itself. `counts`: every block outside the first and the last row of blocks has 4.
All inputs are finite; a program needn't handle non-finite values.
Results may differ from the reference program's by a relative error of at most 0.03.
Values may be sent and summed in bfloat16 or wider, within the bound.
No kernel may reach another device: no remote copies, remote signals or barrier semaphores. Data moves between devices by JAX's collectives and lax.ppermute only.
A program may use at most 64 MiB of HBM per device.

```python
import math
import jax
import jax.numpy as jnp
from jax import lax

HEADS = 12
HEAD_DIM = 64
D = 768
BLK = 8
SLOTS = 4
NBLAT = 8
NBLON = 8
NLAT = 64
NLON = 64
TOKENS = 4096


def draw_queries(key, part):
    return jnp.clip(jax.random.normal(jax.random.fold_in(key, 1), (NLAT, NLON, D), jnp.float32), -6.0, 6.0).astype(jnp.bfloat16)


def draw_key_vectors(key, part):
    return jnp.clip(jax.random.normal(jax.random.fold_in(key, 2), (NLAT, NLON, D), jnp.float32), -6.0, 6.0).astype(jnp.bfloat16)


def neighbour_tables(key):
    base_key = jax.random.fold_in(key, 9)
    step_lat = jnp.array([-1, -1, -1, 0, 0, 1, 1, 1], jnp.int32)
    step_lon = jnp.array([-1, 0, 1, -1, 1, -1, 0, 1], jnp.int32)
    block_lat = jnp.arange(NBLAT, dtype=jnp.int32)[:, None, None]
    block_lon = jnp.arange(NBLON, dtype=jnp.int32)[None, :, None]
    cand_lat = block_lat + step_lat
    cand_lon = (block_lon + step_lon) % NBLON
    inside = (cand_lat >= 0) & (cand_lat < NBLAT)
    ranks = jax.random.randint(jax.random.fold_in(base_key, 1), (NBLAT, NBLON, 8), 0, 4096) * 8 + jnp.arange(8, dtype=jnp.int32)
    ranks = jnp.where(inside, ranks, 65536 + jnp.arange(8, dtype=jnp.int32))
    order = jnp.argsort(ranks, axis=-1)
    cand_index = jnp.broadcast_to(cand_lat * NBLON + cand_lon, (NBLAT, NBLON, 8))
    chosen = jnp.take_along_axis(cand_index, order[:, :, :SLOTS - 1], axis=-1)
    own_index = jnp.broadcast_to(block_lat * NBLON + block_lon, (NBLAT, NBLON, 1))
    polar = (block_lat[:, :, 0] == 0) | (block_lat[:, :, 0] == NBLAT - 1)
    drawn_counts = jax.random.randint(jax.random.fold_in(base_key, 2), (NBLAT, NBLON), 2, SLOTS + 1)
    slot_counts = jnp.where(polar, drawn_counts, SLOTS)
    slot_table = jnp.concatenate([own_index, chosen], axis=-1)
    slot_ids = jnp.arange(SLOTS, dtype=jnp.int32)
    slot_table = jnp.where(slot_ids[None, None, :] < slot_counts[:, :, None], slot_table, own_index)
    return (slot_table.astype(jnp.int32), slot_counts.astype(jnp.int32))


def draw_neighbours(key, part):
    return neighbour_tables(key)[0]


def draw_counts(key, part):
    return neighbour_tables(key)[1]


def levels(key, dims, shards, least, top_value):
    level = 1.0
    for dim, blocks in shards:
        draws = jax.random.uniform(jax.random.fold_in(jax.random.fold_in(key, 6), dim), (blocks,), jnp.float32, least / len(shards), top_value / len(shards))
        level = level * jnp.repeat(jnp.exp(draws), dims[dim] // blocks).reshape((-1,) + (1,) * (len(dims) - 1 - dim))
    return level


def bell_draw(own_key, extent, spread, reach, shards=(), held_as=jnp.bfloat16):
    values = jax.random.normal(own_key, extent, jnp.float32) * spread
    if len(shards) > 0:
        values = levels(own_key, extent, shards, -0.22, 0.18) * values
    return jnp.clip(values, min=-reach, max=reach).astype(held_as)


def setup_inputs(seed: int = 0) -> dict:
    splits = jax.random.split(jax.random.key(seed), 8)
    return {
        "queries": draw_queries(jax.random.fold_in(splits[7], 71), 0),
        "key_vectors": draw_key_vectors(jax.random.fold_in(splits[7], 71), 0),
        "value_vectors": bell_draw(splits[2], (NLAT, NLON, D), 2.0, 12.0, ((0, 4), (1, 8))),
        "upstream": bell_draw(splits[3], (NLAT, NLON, D), 1.0, 6.0, ((0, 4), (1, 8))),
        "w_out": bell_draw(splits[4], (D, D), D ** -0.5, 0.21875),
        "neighbours": draw_neighbours(jax.random.fold_in(splits[7], 71), 0),
        "counts": draw_counts(jax.random.fold_in(splits[7], 71), 0),
    }


def to_blocks(token_grid):
    lat_rows, lon_cols, feat_width = token_grid.shape
    block_tiles = token_grid.reshape(lat_rows // BLK, BLK, lon_cols // BLK, BLK, feat_width).transpose(0, 2, 1, 3, 4)
    return block_tiles.reshape(lat_rows // BLK, lon_cols // BLK, BLK * BLK, feat_width)

def from_blocks(block_tiles):
    lat_blocks, lon_blocks, inner_count, feat_width = block_tiles.shape
    token_grid = block_tiles.reshape(lat_blocks, lon_blocks, BLK, BLK, feat_width).transpose(0, 2, 1, 3, 4)
    return token_grid.reshape(lat_blocks * BLK, lon_blocks * BLK, feat_width)

def heads_of(block_tiles):
    return block_tiles.astype(jnp.float32).reshape(block_tiles.shape[0], block_tiles.shape[1], HEADS, HEAD_DIM)

def row_pass(query_tiles, key_sets, value_sets, key_valid, grad_tiles, w_out):
    score_scale = 1.0 / math.sqrt(HEAD_DIM)
    raw = jnp.einsum('nqhd,nkhd->nhqk', heads_of(query_tiles), heads_of(key_sets)) * score_scale
    masked = jnp.where(key_valid[:, None, None, :], raw, -jnp.inf)
    row_top = lax.optimization_barrier(jnp.max(masked, axis=-1, keepdims=True))
    log_total = row_top + jnp.log(lax.optimization_barrier(jnp.sum(jnp.exp(masked - row_top), axis=-1, keepdims=True)))
    attn_probs = jnp.exp(masked - log_total)
    probs_low = attn_probs.astype(jnp.bfloat16)
    attended = jnp.einsum('nhqk,nkhd->nqhd', probs_low.astype(jnp.float32), heads_of(value_sets))
    attended = attended.astype(jnp.bfloat16).reshape(query_tiles.shape)
    feat_width = query_tiles.shape[-1]
    mixed_row = jnp.dot(attended.reshape(-1, feat_width), w_out, preferred_element_type=jnp.float32).astype(jnp.bfloat16)
    d_att = jnp.dot(grad_tiles.reshape(-1, feat_width), w_out.T, preferred_element_type=jnp.float32).astype(jnp.bfloat16)
    d_att = d_att.reshape(query_tiles.shape)
    row_delta = lax.optimization_barrier(jnp.sum(heads_of(d_att) * heads_of(attended), axis=-1)).transpose(0, 2, 1)
    dprobs = jnp.einsum('nqhd,nkhd->nhqk', heads_of(d_att), heads_of(value_sets))
    dscores = (attn_probs * (dprobs - row_delta[..., None]) * score_scale).astype(jnp.bfloat16)
    query_grad = jnp.einsum('nhqk,nkhd->nqhd', dscores.astype(jnp.float32), heads_of(key_sets))
    query_grad = query_grad.astype(jnp.bfloat16).reshape(query_tiles.shape)
    key_terms = jnp.einsum('nhqk,nqhd->nkhd', dscores.astype(jnp.float32), heads_of(query_tiles)).reshape(key_sets.shape)
    value_terms = jnp.einsum('nhqk,nqhd->nkhd', probs_low.astype(jnp.float32), heads_of(d_att)).reshape(key_sets.shape)
    return (mixed_row.reshape(query_tiles.shape), query_grad, key_terms, value_terms, attended)

def reference(queries, key_vectors, value_vectors, upstream, w_out, neighbours, counts):
    feat_width = queries.shape[-1]
    query_tiles = to_blocks(queries)
    grad_tiles = to_blocks(upstream)
    key_flat = to_blocks(key_vectors).reshape(NBLAT * NBLON, BLK * BLK, feat_width)
    value_flat = to_blocks(value_vectors).reshape(NBLAT * NBLON, BLK * BLK, feat_width)
    slot_ok = jnp.arange(SLOTS, dtype=jnp.int32)[None, None, :] < counts[:, :, None]

    def row_step(carry, row_inputs):
        key_acc, value_acc = carry
        query_row, grad_row, index_row, ok_row = row_inputs
        flat_index = index_row.reshape(-1).astype(jnp.int32)
        key_sets = jnp.take(key_flat, flat_index, axis=0).reshape(NBLON, SLOTS * BLK * BLK, feat_width)
        value_sets = jnp.take(value_flat, flat_index, axis=0).reshape(NBLON, SLOTS * BLK * BLK, feat_width)
        key_valid = jnp.repeat(ok_row, BLK * BLK, axis=1)
        mixed_row, query_grad, key_terms, value_terms, attended = row_pass(query_row, key_sets, value_sets, key_valid, grad_row, w_out)
        key_acc = key_acc.at[flat_index].add(key_terms.reshape(NBLON * SLOTS, BLK * BLK, feat_width))
        value_acc = value_acc.at[flat_index].add(value_terms.reshape(NBLON * SLOTS, BLK * BLK, feat_width))
        return ((key_acc, value_acc), (mixed_row, query_grad, attended))
    zero_acc = jnp.zeros((NBLAT * NBLON, BLK * BLK, feat_width), jnp.float32)
    (key_acc, value_acc), (mixed_rows, query_rows, attended_rows) = lax.scan(row_step, (zero_acc, zero_acc), (query_tiles, grad_tiles, neighbours, slot_ok))
    w_grad = jnp.dot(attended_rows.reshape(-1, feat_width).T, grad_tiles.reshape(-1, feat_width), preferred_element_type=jnp.float32) / math.sqrt(TOKENS)
    k_grad = from_blocks(key_acc.astype(jnp.bfloat16).reshape(NBLAT, NBLON, BLK * BLK, feat_width))
    v_grad = from_blocks(value_acc.astype(jnp.bfloat16).reshape(NBLAT, NBLON, BLK * BLK, feat_width))
    return (from_blocks(mixed_rows), from_blocks(query_rows), k_grad, v_grad, w_grad)
```

```python
import functools
import math

import jax
import jax.numpy as jnp
from jax import lax
from jax.experimental import pallas as pl
from jax.experimental.pallas import tpu as pltpu
from jax.sharding import PartitionSpec as P

HEAD_DIM = 64
BLK = 8
INNER = BLK * BLK
SLOTS = 4
PAIR = 2 * HEAD_DIM
NEG = -1e30
BOTH = ("lat", "lon")

VMEM = pl.BlockSpec(memory_space=pltpu.VMEM)
SMEM = pl.BlockSpec(memory_space=pltpu.SMEM)


def swap(pairs):
    return [(a, b) for a, b in pairs] + [(b, a) for a, b in pairs]


def slot_places(table, nb, lon_total):
    lat_index, lon_index = table[nb * SLOTS + nb], table[nb * SLOTS + nb + 1]
    even = lax.rem(lon_index, 2) == 0
    places = []
    for q in range(nb):
        row = []
        for s in range(SLOTS):
            block = table[q * SLOTS + s]
            lat_block = block // lon_total
            lon_block = block - lat_block * lon_total
            right = lon_block == lax.rem(lon_index + 1, lon_total)
            side = jnp.where(right == even, 1, 2)
            column = jnp.where(lon_block == lon_index, 0, side)
            row.append(column * (nb + 2) + lat_block - lat_index * nb + 1)
        places.append(row)
    return places


def edge_rows(table, nb):
    even = lax.rem(table[nb * SLOTS + nb], 2) == 0
    return jnp.where(even, nb + 1, 0), jnp.where(even, 0, nb + 1)


def fill(ext, table, nb, own, side_a, side_b, edge_e, edge_f, corner_a, corner_b):
    row_e, row_f = edge_rows(table, nb)
    step = nb + 2
    for kv in range(2):
        for r in range(nb):
            ext[kv, r + 1] = own[kv, r]
            ext[kv, step + r + 1] = side_a[kv, r]
            ext[kv, 2 * step + r + 1] = side_b[kv, r]
        for row, edge, index in ((row_e, edge_e, 0), (row_f, edge_f, 1)):
            ext[kv, row] = edge[kv]
            ext[kv, step + row] = corner_a[index, kv]
            ext[kv, 2 * step + row] = corner_b[index, kv]


def head_masks(value):
    low = lax.broadcasted_iota(jnp.int32, (INNER, PAIR), 1) < HEAD_DIM
    return (
        jnp.where(low, value, 0.0).astype(jnp.bfloat16),
        jnp.where(low, 0.0, value).astype(jnp.bfloat16),
        low,
    )


def two_heads(x, masks):
    return jnp.concatenate([x * masks[0], x * masks[1]], axis=0)


def dot(a, b, dims):
    return lax.dot_general(a, b, (dims, ((), ())), preferred_element_type=jnp.float32)


def probabilities(q2, keys, valid):
    scores = jnp.where(valid, dot(q2, keys, ((1,), (1,))), NEG)
    top = jnp.max(scores, axis=1, keepdims=True)
    weight = jnp.exp(scores - top)
    return weight / jnp.sum(weight, axis=1, keepdims=True)


def key_set(ext, kv, places, cols):
    return jnp.concatenate([ext[kv, place, :, cols] for place in places], axis=0)


def forward_kernel(nb, lon_total, table, q_ref, *refs):
    *inputs, att_ref, ext = refs
    fill(ext, table, nb, *inputs)
    places = slot_places(table, nb, lon_total)
    masks = head_masks(1.0 / math.sqrt(HEAD_DIM))
    low = masks[2]
    slot = lax.broadcasted_iota(jnp.int32, (2 * INNER, SLOTS * INNER), 1) // INNER
    for q in range(nb):
        valid = slot < table[nb * SLOTS + q]
        for p in range(q_ref.shape[-1] // PAIR):
            cols = slice(p * PAIR, (p + 1) * PAIR)
            q2 = two_heads(q_ref[q, :, cols], masks)
            probs = probabilities(q2, key_set(ext, 0, places[q], cols), valid)
            mixed = dot(
                probs.astype(jnp.bfloat16), key_set(ext, 1, places[q], cols), ((1,), (0,))
            )
            att_ref[q, :, cols] = jnp.where(low, mixed[:INNER], mixed[INNER:]).astype(
                jnp.bfloat16
            )


def backward_kernel(nb, lon_total, table, q_ref, da_ref, att_ref, *refs):
    *inputs, dq_ref, own_ref, edge_ref, a_ref, bc_ref, bo_ref, ext, acc = refs
    fill(ext, table, nb, *inputs)
    places = slot_places(table, nb, lon_total)
    scale = 1.0 / math.sqrt(HEAD_DIM)
    masks = head_masks(scale)
    ones = head_masks(1.0)
    low = masks[2]
    slot = lax.broadcasted_iota(jnp.int32, (2 * INNER, SLOTS * INNER), 1) // INNER
    acc[...] = jnp.zeros_like(acc)
    for q in range(nb):
        valid = slot < table[nb * SLOTS + q]
        for p in range(q_ref.shape[-1] // PAIR):
            cols = slice(p * PAIR, (p + 1) * PAIR)
            q2 = two_heads(q_ref[q, :, cols], masks)
            keys = key_set(ext, 0, places[q], cols)
            values = key_set(ext, 1, places[q], cols)
            probs = probabilities(q2, keys, valid)
            da = da_ref[q, :, cols]
            da2 = two_heads(da, ones)
            product = da.astype(jnp.float32) * att_ref[q, :, cols].astype(jnp.float32)
            delta = jnp.concatenate(
                [
                    jnp.sum(jnp.where(low, product, 0.0), axis=1, keepdims=True),
                    jnp.sum(jnp.where(low, 0.0, product), axis=1, keepdims=True),
                ],
                axis=0,
            )
            dprobs = dot(da2, values, ((1,), (1,)))
            dscores = (probs * (dprobs - delta)).astype(jnp.bfloat16)
            dq2 = dot(dscores, keys, ((1,), (0,)))
            dq_ref[q, :, cols] = (jnp.where(low, dq2[:INNER], dq2[INNER:]) * scale).astype(
                jnp.bfloat16
            )
            dk = dot(dscores, q2, ((0,), (0,)))
            dv = dot(probs.astype(jnp.bfloat16), da2, ((0,), (0,)))
            for s in range(SLOTS):
                rows = slice(s * INNER, (s + 1) * INNER)
                acc[0, places[q][s], :, cols] += dk[rows]
                acc[1, places[q][s], :, cols] += dv[rows]
    row_e, row_f = edge_rows(table, nb)
    step = nb + 2
    for kv in range(2):
        for r in range(nb):
            own_ref[kv, r] = acc[kv, r + 1]
            a_ref[kv, r] = acc[kv, step + r + 1].astype(jnp.bfloat16)
            bo_ref[kv, r] = acc[kv, 2 * step + r + 1].astype(jnp.bfloat16)
        for index, row in ((0, row_e), (1, row_f)):
            edge_ref[index, kv] = acc[kv, row]
            a_ref[kv, nb + index] = acc[kv, step + row].astype(jnp.bfloat16)
            bc_ref[index, kv] = acc[kv, 2 * step + row].astype(jnp.bfloat16)


def weight_kernel(bits, att_own, att_other, up_own, up_other, send_ref, keep_ref):
    half = att_own.shape[1] // 2
    cols = pl.ds(pl.multiple_of(bits[0] * half, half), half)
    total = dot(att_own[:, cols], up_own[...], ((0,), (0,)))
    total += dot(att_other[:, cols], up_other[...], ((0,), (0,)))
    rows = half // 2
    first = bits[1] == 0
    keep_ref[...] = jnp.where(first, total[:rows], total[rows:])
    send_ref[...] = jnp.where(first, total[rows:], total[:rows]).astype(jnp.bfloat16)


def flips(size):
    assert size & (size - 1) == 0
    return [1 << k for k in range(size.bit_length() - 1)]


def sum_over_mesh(att, upstream, up_other, att_other, lat_size, lon_size):
    lat_index, lon_index = lax.axis_index("lat"), lax.axis_index("lon")
    core = lon_index % 2
    lat_flips, lon_flips = flips(lat_size), flips(lon_size)[1:]
    lat_orders = (lat_flips, lat_flips[::-1])
    lon_orders = (lon_flips, lon_flips[::-1])

    def exchange(value, step, on_lat):
        pairs = []
        for a in range(lat_size):
            for o in range(lon_size):
                if on_lat:
                    to = (a ^ lat_orders[o % 2][step], o)
                else:
                    to = (a, o ^ lon_orders[o % 2][step])
                pairs.append((a * lon_size + o, to[0] * lon_size + to[1]))
        return lax.ppermute(value, BOTH, pairs)

    sides = [
        (lat_index // jnp.where(core == 0, one, two)) % 2 for one, two in zip(*lat_orders)
    ]
    width = att.shape[1]
    rows = width // 4
    send, total = pl.pallas_call(
        weight_kernel,
        out_shape=(
            jax.ShapeDtypeStruct((rows, width), jnp.bfloat16),
            jax.ShapeDtypeStruct((rows, width), jnp.float32),
        ),
        in_specs=[SMEM] + [VMEM] * 4,
        out_specs=(VMEM, VMEM),
        name="weight",
    )(jnp.stack([core, sides[0]]).astype(jnp.int32), att, att_other, upstream, up_other)
    total = total + exchange(send, 0, True).astype(jnp.float32)
    for step in range(1, len(lat_flips)):
        halves = total.reshape(2, -1, width)
        keep = lax.dynamic_index_in_dim(halves, sides[step], 0, keepdims=False)
        send = lax.dynamic_index_in_dim(halves, 1 - sides[step], 0, keepdims=False)
        got = exchange(send.astype(jnp.bfloat16), step, True)
        total = keep + got.astype(jnp.float32)
    low = total.astype(jnp.bfloat16)
    for step in range(len(lon_flips)):
        got = exchange(low, step, False)
        low = (low.astype(jnp.float32) + got.astype(jnp.float32)).astype(jnp.bfloat16)
    for step in reversed(range(len(lat_flips))):
        got = exchange(low, step, True)
        mine = lax.broadcasted_iota(jnp.int32, (2, 1, 1), 0) == sides[step]
        low = jnp.where(mine, low[None], got[None]).reshape(-1, width)
    other = lax.ppermute(low, "lon", swap([(o, o + 1) for o in range(0, lon_size, 2)]))
    mine = lax.broadcasted_iota(jnp.int32, (2, 1, 1), 0) == core
    return jnp.where(mine, low[None], other[None]).reshape(width, width).astype(jnp.float32)


def on_device(queries, key_vectors, value_vectors, upstream, w_out, neighbours, counts):
    lat_rows, lon_cols, width = queries.shape
    assert lon_cols == BLK
    nb = lat_rows // BLK
    lat_size, lon_size = lax.axis_size("lat"), lax.axis_size("lon")
    lat_index, lon_index = lax.axis_index("lat"), lax.axis_index("lon")
    lon_total = neighbours.shape[1]
    even = lat_index % 2 == 0
    pairs_a = swap([(o, o + 1) for o in range(0, lon_size, 2)])
    pairs_b = swap([(o, (o + 1) % lon_size) for o in range(1, lon_size, 2)])
    pairs_e = swap([(a, a + 1) for a in range(0, lat_size, 2)])
    pairs_f = swap([(a, a + 1) for a in range(1, lat_size - 1, 2)])

    blocks = (nb, INNER, width)
    kv = jnp.stack([key_vectors.reshape(blocks), value_vectors.reshape(blocks)])
    q_tiles = queries.reshape(blocks)
    edge = jnp.where(even, nb - 1, 0)

    side_b = lax.ppermute(kv, "lon", pairs_b)
    send_e = lax.dynamic_index_in_dim(kv, edge, 1, keepdims=False)
    send_f = lax.dynamic_index_in_dim(kv, nb - 1 - edge, 1, keepdims=False)
    edge_e = lax.ppermute(send_e, "lat", pairs_e)
    edge_f = lax.ppermute(send_f, "lat", pairs_f)
    side_a = lax.ppermute(kv, "lon", pairs_a)
    edges = jnp.stack([edge_e, edge_f])
    corner_b = lax.ppermute(edges, "lon", pairs_b)
    corner_a = lax.ppermute(edges, "lon", pairs_a)
    up_flat = upstream.reshape(-1, width)
    up_other = lax.ppermute(up_flat, "lon", pairs_a)

    slots = lax.dynamic_slice(neighbours, (lat_index * nb, lon_index, 0), (nb, 1, SLOTS))
    limits = lax.dynamic_slice(counts, (lat_index * nb, lon_index), (nb, 1))
    table = jnp.concatenate(
        [slots.reshape(-1), limits.reshape(-1), jnp.stack([lat_index, lon_index])]
    )
    d_att = dot(up_flat, w_out, ((1,), (1,))).astype(jnp.bfloat16)

    extended = (kv, side_a, side_b, edge_e, edge_f, corner_a, corner_b)
    ext = pltpu.VMEM((2, 3 * (nb + 2), INNER, width), jnp.bfloat16)
    att = pl.pallas_call(
        functools.partial(forward_kernel, nb, lon_total),
        out_shape=jax.ShapeDtypeStruct(blocks, jnp.bfloat16),
        in_specs=[SMEM] + [VMEM] * 8,
        out_specs=VMEM,
        scratch_shapes=[ext],
        name="forward",
    )(table, q_tiles, *extended)
    att_flat = att.reshape(-1, width)
    att_other = lax.ppermute(att_flat, "lon", pairs_a)
    w_sum = sum_over_mesh(att_flat, up_flat, up_other, att_other, lat_size, lon_size)
    tokens = lat_rows * lon_cols * lat_size * lon_size
    w_grad = w_sum * (1.0 / math.sqrt(tokens))

    low, full = jnp.bfloat16, jnp.float32
    q_grad, own, edge_sum, back_a, back_bc, back_bo = pl.pallas_call(
        functools.partial(backward_kernel, nb, lon_total),
        out_shape=(
            jax.ShapeDtypeStruct(blocks, low),
            jax.ShapeDtypeStruct((2,) + blocks, full),
            jax.ShapeDtypeStruct((2, 2, INNER, width), full),
            jax.ShapeDtypeStruct((2, nb + 2, INNER, width), low),
            jax.ShapeDtypeStruct((2, 2, INNER, width), low),
            jax.ShapeDtypeStruct((2,) + blocks, low),
        ),
        in_specs=[SMEM] + [VMEM] * 10,
        out_specs=(VMEM,) * 6,
        scratch_shapes=[ext, pltpu.VMEM((2, 3 * (nb + 2), INNER, width), full)],
        name="backward",
    )(table, q_tiles, d_att.reshape(blocks), att, *extended)
    mixed = dot(att_flat, w_out, ((1,), (0,))).astype(low)

    got_bc = lax.ppermute(back_bc, "lon", pairs_b)
    got_a = lax.ppermute(back_a, "lon", pairs_a)
    got_bo = lax.ppermute(back_bo, "lon", pairs_b)
    edge_sum = edge_sum + got_bc.astype(full)
    edge_sum = edge_sum + jnp.swapaxes(got_a[:, nb:], 0, 1).astype(full)
    edge_sum = edge_sum.astype(low)
    got_e = lax.ppermute(edge_sum[0], "lat", pairs_e)
    got_f = lax.ppermute(edge_sum[1], "lat", pairs_f)
    total = own + got_a[:, :nb].astype(full) + got_bo.astype(full)
    row = lax.broadcasted_iota(jnp.int32, (1, nb, 1, 1), 1)
    total = total + jnp.where(row == edge, got_e[:, None].astype(full), 0.0)
    total = total + jnp.where(row == nb - 1 - edge, got_f[:, None].astype(full), 0.0)
    total = total.astype(low)
    shape = queries.shape
    return (
        mixed.reshape(shape),
        q_grad.reshape(shape),
        total[0].reshape(shape),
        total[1].reshape(shape),
        w_grad,
    )


def solution(mesh):
    grid = P("lat", "lon", None)
    return jax.shard_map(
        on_device,
        mesh=mesh,
        in_specs=(grid, grid, grid, grid, P(), P(), P()),
        out_specs=(grid, grid, grid, grid, P()),
        check_vma=False,
    )
```

```python
import functools
import math

import jax
import jax.numpy as jnp
from jax import lax
from jax.experimental import pallas as pl
from jax.experimental.pallas import tpu as pltpu
from jax.sharding import PartitionSpec as P


HEAD_DIM = 64
BLK = 8
INNER = BLK * BLK
SLOTS = 4
PAIR = 2 * HEAD_DIM
STAT = 16
NEG = -1e30
BOTH = ("lat", "lon")

VMEM = pl.BlockSpec(memory_space=pltpu.VMEM)
SMEM = pl.BlockSpec(memory_space=pltpu.SMEM)


def swap(pairs):
    return [(a, b) for a, b in pairs] + [(b, a) for a, b in pairs]


def places_of(info, nb, lon_total, neighbours):
    lat_index, lon_index = info[0], info[1]
    even = lax.rem(lon_index, 2) == 0
    places = []
    for q in range(nb):
        row = []
        for s in range(SLOTS):
            block = neighbours[lat_index * nb + q, lon_index, s]
            lat_block = block // lon_total
            lon_block = block - lat_block * lon_total
            right = lon_block == lax.rem(lon_index + 1, lon_total)
            side = jnp.where(right == even, 1, 2)
            column = jnp.where(lon_block == lon_index, 0, side)
            row.append(column * (nb + 2) + lat_block - lat_index * nb + 1)
        places.append(row)
    return places


def edge_rows(info, nb):
    even = lax.rem(info[0], 2) == 0
    return jnp.where(even, nb + 1, 0), jnp.where(even, 0, nb + 1)


def fill(ext, info, nb, parts):
    own, side_a, side_b, edge_e, edge_f, *corners = parts
    if len(corners) == 2:
        corners = [corner.at[k] for corner in corners for k in range(2)]
    e_a, f_a, e_b, f_b = corners
    row_e, row_f = edge_rows(info, nb)
    step = nb + 2
    for i in range(ext.shape[0]):
        for column, rows, e, f in (
            (0, own, edge_e, edge_f),
            (step, side_a, e_a, f_a),
            (2 * step, side_b, e_b, f_b),
        ):
            for r in range(nb):
                ext[i, column + r + 1] = rows[i, r]
            ext[i, column + row_e] = e[i]
            ext[i, column + row_f] = f[i]


def head_masks(value):
    low = lax.broadcasted_iota(jnp.int32, (INNER, PAIR), 1) < HEAD_DIM
    return (
        jnp.where(low, value, 0.0).astype(jnp.bfloat16),
        jnp.where(low, 0.0, value).astype(jnp.bfloat16),
        low,
    )


def two_heads(x, masks):
    return jnp.concatenate([x * masks[0], x * masks[1]], axis=0)


def dot(a, b, dims):
    return lax.dot_general(a, b, (dims, ((), ())), preferred_element_type=jnp.float32)


def probabilities(q2, keys, valid):
    scores = jnp.where(valid, dot(q2, keys, ((1,), (1,))), NEG)
    top = jnp.max(scores, axis=1, keepdims=True)
    weight = jnp.exp(scores - top)
    return weight / jnp.sum(weight, axis=1, keepdims=True)


def key_set(ext, kv, places, cols):
    return jnp.concatenate([ext[kv, place, :, cols] for place in places], axis=0)


def pack_kernel(info, k_ref, v_ref, kv_ref, e_ref, f_ref):
    nb = k_ref.shape[0]
    edge = jnp.where(lax.rem(info[0], 2) == 0, nb - 1, 0)
    for i, ref in enumerate((k_ref, v_ref)):
        kv_ref[i] = ref[...]
        e_ref[i] = ref[edge]
        f_ref[i] = ref[nb - 1 - edge]


def project_kernel(info, q_ref, up_ref, w_ref, qd_ref, e_ref, f_ref):
    nb = q_ref.shape[0]
    edge = jnp.where(lax.rem(info[0], 2) == 0, nb - 1, 0)
    qd_ref[0] = q_ref[...]
    up = up_ref[...].reshape(nb * INNER, -1)
    d_att = dot(up, w_ref[...], ((1,), (1,))).astype(jnp.bfloat16)
    qd_ref[1] = d_att.reshape(nb, INNER, -1)
    for i in range(2):
        e_ref[i] = qd_ref[i, edge]
        f_ref[i] = qd_ref[i, nb - 1 - edge]


def key_slots():
    return lax.broadcasted_iota(jnp.int32, (2 * INNER, SLOTS * INNER), 1) // INNER


def forward_kernel(nb, lon_total, info, neighbours, counts, qd_ref, *refs):
    *inputs, att_ref, stats_ref, ext = refs
    fill(ext, info, nb, inputs)
    places = places_of(info, nb, lon_total, neighbours)
    masks = head_masks(1.0 / math.sqrt(HEAD_DIM))
    low, slot = masks[2], key_slots()
    lane = lax.broadcasted_iota(jnp.int32, (2 * INNER, PAIR), 1)
    stats = jnp.zeros((2 * INNER, PAIR), jnp.float32)
    for q in range(nb):
        valid = slot < counts[info[0] * nb + q, info[1]]
        for p in range(qd_ref.shape[-1] // PAIR):
            cols = slice(p * PAIR, (p + 1) * PAIR)
            q2 = two_heads(qd_ref[0, q, :, cols], masks)
            scores = dot(q2, key_set(ext, 0, places[q], cols), ((1,), (1,)))
            scores = jnp.where(valid, scores, NEG)
            top = jnp.max(scores, axis=1, keepdims=True)
            weight = jnp.exp(scores - top)
            total = jnp.sum(weight, axis=1, keepdims=True)
            probs = (weight / total).astype(jnp.bfloat16)
            mixed = dot(probs, key_set(ext, 1, places[q], cols), ((1,), (0,)))
            att = jnp.where(low, mixed[:INNER], mixed[INNER:]).astype(jnp.bfloat16)
            att_ref[q, :, cols] = att
            product = qd_ref[1, q, :, cols].astype(jnp.float32) * att.astype(jnp.float32)
            delta = row_sums(product, low)
            stats = jnp.where(lane == q * STAT + p, top + jnp.log(total), stats)
            stats = jnp.where(lane == q * STAT + STAT // 2 + p, delta, stats)
    flipped = stats.T
    for q in range(nb):
        stats_ref[0, q] = flipped[q * STAT : (q + 1) * STAT]


def row_sums(product, low):
    return jnp.concatenate(
        [
            jnp.sum(jnp.where(low, product, 0.0), axis=1, keepdims=True),
            jnp.sum(jnp.where(low, 0.0, product), axis=1, keepdims=True),
        ],
        axis=0,
    )


def query_kernel(nb, lon_total, info, neighbours, counts, qd_ref, att_ref, *refs):
    *inputs, dq_ref, ext = refs
    fill(ext, info, nb, inputs)
    places = places_of(info, nb, lon_total, neighbours)
    scale = 1.0 / math.sqrt(HEAD_DIM)
    masks, ones = head_masks(scale), head_masks(1.0)
    low, slot = masks[2], key_slots()
    for q in range(nb):
        valid = slot < counts[info[0] * nb + q, info[1]]
        for p in range(qd_ref.shape[-1] // PAIR):
            cols = slice(p * PAIR, (p + 1) * PAIR)
            q2 = two_heads(qd_ref[0, q, :, cols], masks)
            keys = key_set(ext, 0, places[q], cols)
            values = key_set(ext, 1, places[q], cols)
            probs = probabilities(q2, keys, valid)
            da = qd_ref[1, q, :, cols]
            product = da.astype(jnp.float32) * att_ref[q, :, cols].astype(jnp.float32)
            dprobs = dot(two_heads(da, ones), values, ((1,), (1,)))
            dscores = (probs * (dprobs - row_sums(product, low))).astype(jnp.bfloat16)
            dq2 = dot(dscores, keys, ((1,), (0,)))
            dq_ref[q, :, cols] = (jnp.where(low, dq2[:INNER], dq2[INNER:]) * scale).astype(
                jnp.bfloat16
            )


def key_kernel(nb, lon_total, info, neighbours, counts, kv_ref, *refs):
    *inputs, dk_ref, dv_ref, ext, stats, acc = refs
    fill(ext, info, nb, inputs[:7])
    fill(stats, info, nb, inputs[7:])
    masks, ones = head_masks(1.0 / math.sqrt(HEAD_DIM)), head_masks(1.0)
    lat_index, lon_index = info[0], info[1]
    lat_total = neighbours.shape[0]
    forward = jnp.where(lax.rem(lon_index, 2) == 0, 1, lon_total - 1)
    acc[...] = jnp.zeros_like(acc)
    columns = 3 if lon_total > 2 else 2

    def visit(n, carry):
        r = n // (3 * columns)
        place = n - r * (3 * columns)
        column = place // 3
        row = r + place - column * 3
        shift = jnp.where(column == 0, 0, jnp.where(column == 1, forward, lon_total - forward))
        lon_block = lax.rem(lon_index + shift, lon_total)
        lat_block = lat_index * nb + row - 1
        safe = jnp.clip(lat_block, 0, lat_total - 1)
        key_id = (lat_index * nb + r) * lon_total + lon_index
        limit = counts[safe, lon_block]
        hit = neighbours[safe, lon_block, 0] == key_id
        for s in range(1, SLOTS):
            hit |= (neighbours[safe, lon_block, s] == key_id) & (s < limit)

        @pl.when(hit & (safe == lat_block))
        def _():
            index = column * (nb + 2) + row
            for p in range(kv_ref.shape[-1] // PAIR):
                cols = slice(p * PAIR, (p + 1) * PAIR)
                q2 = two_heads(ext[0, index, :, cols], masks)
                da2 = two_heads(ext[1, index, :, cols], ones)
                scores = dot(kv_ref[0, r, :, cols], q2, ((1,), (1,)))
                probs = jnp.exp(scores - stats[0, index, p : p + 1, :])
                dprobs = dot(kv_ref[1, r, :, cols], da2, ((1,), (1,)))
                delta = stats[0, index, STAT // 2 + p : STAT // 2 + p + 1, :]
                dscores = (probs * (dprobs - delta)).astype(jnp.bfloat16)
                acc[0, r, :, cols] += dot(dscores, q2, ((1,), (0,)))
                acc[1, r, :, cols] += dot(probs.astype(jnp.bfloat16), da2, ((1,), (0,)))

        return carry

    lax.fori_loop(0, nb * 3 * columns, visit, 0)
    dk_ref[...] = acc[0].astype(jnp.bfloat16)
    dv_ref[...] = acc[1].astype(jnp.bfloat16)


def weight_kernel(info, att_own, att_other, up_own, up_other, send_ref, keep_ref):
    half = att_own.shape[1] // 2
    cols = pl.ds(pl.multiple_of(lax.rem(info[1], 2) * half, half), half)
    total = dot(att_own[:, cols], up_own[...], ((0,), (0,)))
    total += dot(att_other[:, cols], up_other[...], ((0,), (0,)))
    rows = half // 2
    first = info[2] == 0
    keep_ref[...] = jnp.where(first, total[:rows], total[rows:])
    send_ref[...] = jnp.where(first, total[rows:], total[:rows]).astype(jnp.bfloat16)


def finish_kernel(scale, info, own_ref, other_ref, out_ref):
    half = own_ref.shape[0]
    core = lax.rem(info[1], 2)
    for ref, at in ((own_ref, core), (other_ref, 1 - core)):
        rows = pl.ds(pl.multiple_of(at * half, half), half)
        out_ref[rows, :] = ref[...].astype(jnp.float32) * scale


def flips(size):
    assert size & (size - 1) == 0
    return [1 << k for k in range(size.bit_length() - 1)]


def lat_sides(lat_size):
    bits = flips(lat_size)
    lat_index, core = lax.axis_index("lat"), lax.axis_index("lon") % 2
    return [
        (lat_index // jnp.where(core == 0, one, two)) % 2 for one, two in zip(bits, bits[::-1])
    ]


def sum_over_mesh(info, sides, att, upstream, up_other, att_other, lat_size, lon_size, scale):
    lat_flips, lon_flips = flips(lat_size), flips(lon_size)[1:]
    lat_orders = (lat_flips, lat_flips[::-1])
    lon_orders = (lon_flips, lon_flips[::-1])

    def exchange(value, step, on_lat):
        pairs = []
        for a in range(lat_size):
            for o in range(lon_size):
                if on_lat:
                    to = (a ^ lat_orders[o % 2][step], o)
                else:
                    to = (a, o ^ lon_orders[o % 2][step])
                pairs.append((a * lon_size + o, to[0] * lon_size + to[1]))
        return lax.ppermute(value, BOTH, pairs)

    width = att.shape[1]
    rows = width // 4
    send, total = pl.pallas_call(
        weight_kernel,
        out_shape=(
            jax.ShapeDtypeStruct((rows, width), jnp.bfloat16),
            jax.ShapeDtypeStruct((rows, width), jnp.float32),
        ),
        in_specs=[SMEM] + [VMEM] * 4,
        out_specs=(VMEM, VMEM),
        name="weight",
    )(info, att, att_other, upstream, up_other)
    got = exchange(send, 0, True)
    for step in range(1, len(lat_flips)):
        total = total + got.astype(jnp.float32)
        halves = total.reshape(2, -1, width)
        total = lax.dynamic_index_in_dim(halves, sides[step], 0, keepdims=False)
        send = lax.dynamic_index_in_dim(halves, 1 - sides[step], 0, keepdims=False)
        got = exchange(send.astype(jnp.bfloat16), step, True)
    low = (total + got.astype(jnp.float32)).astype(jnp.bfloat16)
    for step in range(len(lon_flips)):
        got = exchange(low, step, False)
        low = (low.astype(jnp.float32) + got.astype(jnp.float32)).astype(jnp.bfloat16)
    for step in reversed(range(len(lat_flips))):
        got = exchange(low, step, True)
        mine = lax.broadcasted_iota(jnp.int32, (2, 1, 1), 0) == sides[step]
        low = jnp.where(mine, low[None], got[None]).reshape(-1, width)
    other = lax.ppermute(low, "lon", swap([(o, o + 1) for o in range(0, lon_size, 2)]))
    return pl.pallas_call(
        functools.partial(finish_kernel, scale),
        out_shape=jax.ShapeDtypeStruct((width, width), jnp.float32),
        in_specs=[SMEM, VMEM, VMEM],
        out_specs=VMEM,
        name="finish",
    )(info, low, other)


def layer(queries, key_vectors, value_vectors, upstream, w_out, neighbours, counts):
    lat_rows, lon_cols, width = queries.shape
    assert lon_cols == BLK
    nb = lat_rows // BLK
    lat_size, lon_size = lax.axis_size("lat"), lax.axis_size("lon")
    lon_total = neighbours.shape[1]
    pairs_a = swap([(o, o + 1) for o in range(0, lon_size, 2)])
    pairs_b = swap([(o, (o + 1) % lon_size) for o in range(1, lon_size, 2)])
    pairs_e = swap([(a, a + 1) for a in range(0, lat_size, 2)])
    pairs_f = swap([(a, a + 1) for a in range(1, lat_size - 1, 2)])
    low, full = jnp.bfloat16, jnp.float32
    blocks = (nb, INNER, width)

    def spread(own, to_e, to_f, joined=True):
        side_b = lax.ppermute(own, "lon", pairs_b)
        edge_e = lax.ppermute(to_e, "lat", pairs_e)
        edge_f = lax.ppermute(to_f, "lat", pairs_f)
        side_a = lax.ppermute(own, "lon", pairs_a)
        if joined:
            edges = jnp.stack([edge_e, edge_f])
            corner_b = lax.ppermute(edges, "lon", pairs_b)
            corner_a = lax.ppermute(edges, "lon", pairs_a)
            return (own, side_a, side_b, edge_e, edge_f, corner_a, corner_b)
        e_b = lax.ppermute(edge_e, "lon", pairs_b)
        f_b = lax.ppermute(edge_f, "lon", pairs_b)
        e_a = lax.ppermute(edge_e, "lon", pairs_a)
        f_a = lax.ppermute(edge_f, "lon", pairs_a)
        return (own, side_a, side_b, edge_e, edge_f, e_a, f_a, e_b, f_b)

    sides = lat_sides(lat_size)
    info = jnp.stack([lax.axis_index("lat"), lax.axis_index("lon"), sides[0]]).astype(jnp.int32)
    packed = (
        jax.ShapeDtypeStruct((2,) + blocks, low),
        jax.ShapeDtypeStruct((2,) + blocks[1:], low),
        jax.ShapeDtypeStruct((2,) + blocks[1:], low),
    )
    kv = pl.pallas_call(
        pack_kernel,
        out_shape=packed,
        in_specs=[SMEM, VMEM, VMEM],
        out_specs=(VMEM,) * 3,
        name="pack",
    )(info, key_vectors.reshape(blocks), value_vectors.reshape(blocks))
    kv = spread(*kv, joined=False)
    up_flat = upstream.reshape(-1, width)
    qd = pl.pallas_call(
        project_kernel,
        out_shape=packed,
        in_specs=[SMEM] + [VMEM] * 3,
        out_specs=(VMEM,) * 3,
        name="project",
    )(info, queries.reshape(blocks), upstream.reshape(blocks), w_out)
    up_other = lax.ppermute(up_flat, "lon", pairs_a)
    qd_all = spread(*qd)

    scalars = (info, neighbours, counts)
    ext = pltpu.VMEM((2, 3 * (nb + 2), INNER, width), low)
    att, stats = pl.pallas_call(
        functools.partial(forward_kernel, nb, lon_total),
        out_shape=(
            jax.ShapeDtypeStruct(blocks, low),
            jax.ShapeDtypeStruct((1, nb, STAT, PAIR), full),
        ),
        in_specs=[SMEM] * 3 + [VMEM] * 10,
        out_specs=(VMEM, VMEM),
        scratch_shapes=[ext],
        name="forward",
    )(*scalars, qd[0], *kv)
    att_flat = att.reshape(-1, width)
    att_other = lax.ppermute(att_flat, "lon", pairs_a)
    tokens = lat_rows * lon_cols * lat_size * lon_size
    w_grad = sum_over_mesh(
        info,
        sides,
        att_flat,
        up_flat,
        up_other,
        att_other,
        lat_size,
        lon_size,
        1.0 / math.sqrt(tokens),
    )
    q_grad = pl.pallas_call(
        functools.partial(query_kernel, nb, lon_total),
        out_shape=jax.ShapeDtypeStruct(blocks, low),
        in_specs=[SMEM] * 3 + [VMEM] * 11,
        out_specs=VMEM,
        scratch_shapes=[ext],
        name="query",
    )(*scalars, qd[0], att, *kv)
    mixed = dot(att_flat, w_out, ((1,), (0,))).astype(low)

    edge = jnp.where(lax.axis_index("lat") % 2 == 0, nb - 1, 0)
    stats_e = lax.dynamic_index_in_dim(stats, edge, 1, keepdims=False)
    stats_f = lax.dynamic_index_in_dim(stats, nb - 1 - edge, 1, keepdims=False)
    stats_all = spread(stats, stats_e, stats_f)
    k_grad, v_grad = pl.pallas_call(
        functools.partial(key_kernel, nb, lon_total),
        out_shape=(jax.ShapeDtypeStruct(blocks, low),) * 2,
        in_specs=[SMEM] * 3 + [VMEM] * 15,
        out_specs=(VMEM, VMEM),
        scratch_shapes=[
            ext,
            pltpu.VMEM((1, 3 * (nb + 2), STAT, PAIR), full),
            pltpu.VMEM((2,) + blocks, full),
        ],
        name="keys",
    )(*scalars, kv[0], *qd_all, *stats_all)
    shape = queries.shape
    return (
        mixed.reshape(shape),
        q_grad.reshape(shape),
        k_grad.reshape(shape),
        v_grad.reshape(shape),
        w_grad,
    )


def solution(mesh):
    grid = P("lat", "lon", None)
    return jax.shard_map(
        layer,
        mesh=mesh,
        in_specs=(grid, grid, grid, grid, P(), P(), P()),
        out_specs=(grid, grid, grid, grid, P()),
        check_vma=False,
    )
```
